32 devices in a mesh: pert: 2 (over y), ga: 4 (over z), band: 4 (over x, core).
Axes of the slice: x: 2, y: 2, z: 4, core: 2. Of those that a mesh axis runs over, the one named last changes fastest.
Arguments:
- psi: float32 [2, 4, 131072], P(None, 'band', 'ga'), may hold values from -6 to 6
- potential: float32 [256, 128, 128], P('pert', 'ga'), parts along dimension 0, may hold values from 1 to 3
- miller: int32 [131072], replicated, may hold values from 0 to 2097151, as said below
- occupied: int32 [4], replicated, may hold values 0 or 1
Outputs:
- projected: float32 [2, 8, 131072], P(None, ('pert', 'band'), 'ga'), parts along dimension 1
The draws below stay inside these ranges and needn't reach their ends.
There are 2 independent parts, one for each index of `pert`. The reference program is written for one: setup_inputs(seed, part) draws one part's arguments, and reference() takes and returns one part's arrays. A program takes and returns all parts, laid end to end along the dimension named above; an argument that names none is the same for every part. Nothing has to cross between parts.
Inputs may be any that keep to these rules, and one draw needn't show every extreme that they name: `miller`: entry k is the flat index a 128^2 + b * 128 + c of coefficient k, with Fourier indices a, b, c in 0..127 taken modulo 128; the entries are distinct; each of a, b, c, read as a signed index in -64..128/2-1, lies in -32..128/4-1; the j-th block of 32768 entries holds only points whose signed a plus 128/4 is congruent to j modulo 131072/32768.
All inputs are finite; a program needn't handle non-finite values.
Results may differ from the reference program's by a relative error of at most 0.00013.
Values sent between devices are 32-bit elements; how exact they have to be, the bound alone decides.
A program may use at most 64 MiB of HBM per device.

```python
import jax
import jax.numpy as jnp
from jax import lax

N = 128
NPW = 131072
NB = 4
PW_SHARD = 32768


def draw_miller(key, part):
    owners = NPW // PW_SHARD
    quarter = N // 4
    per_owner = N * N * N // owners
    slot_index = jnp.arange(per_owner, dtype=jnp.int32)
    owner_index = jnp.arange(owners, dtype=jnp.int32)[:, None]
    plane_index = slot_index // (N * N)
    remainder = slot_index % (N * N)
    row_index = remainder // N
    column_index = remainder % N
    plane_pos = owner_index + owners * plane_index
    signed_a = plane_pos - quarter
    signed_b = row_index - quarter
    signed_c = column_index - quarter
    inside = (plane_pos < N // 2) & (row_index < N // 2)[None, :] & (column_index < N // 2)[None, :]
    radius = signed_a * signed_a + (signed_b * signed_b + signed_c * signed_c)[None, :]
    limit = 2 ** 31 // per_owner - 1
    keys = jax.random.split(key, owners)
    breaker = jax.vmap(lambda sub_key: jax.random.permutation(sub_key, per_owner))(keys).astype(jnp.int32)
    score = jnp.where(inside, jnp.minimum(radius, limit - 1), limit) * per_owner + breaker
    order = jnp.argsort(score, axis=1)[:, :PW_SHARD]
    unsigned_a = (plane_pos + N - quarter) % N
    unsigned_b = (row_index + N - quarter) % N
    unsigned_c = (column_index + N - quarter) % N
    flat_index = unsigned_a * (N * N) + (unsigned_b * N + unsigned_c)[None, :]
    return jnp.take_along_axis(flat_index, order, axis=1).reshape(NPW).astype(jnp.int32)


def plant(values, stream_key, low, largest):
    index_at = [jax.random.randint(jax.random.fold_in(stream_key, axis), (), 0, length) for axis, length in enumerate(values.shape)]
    longest = values.shape.index(max(values.shape))
    neighbour = index_at[:longest] + [(index_at[longest] + 1) % values.shape[longest]] + index_at[longest + 1:]
    return values.at[tuple(index_at)].set(low).at[tuple(neighbour)].set(largest)


def levels(key, extent, cuts, low, high):
    def one(axis_at, parts):
        steps = jax.random.uniform(jax.random.fold_in(jax.random.fold_in(key, 6), axis_at), (parts,), jnp.float32, low / len(cuts), high / len(cuts))
        return jnp.repeat(jnp.exp(steps), extent[axis_at] // parts).reshape((-1,) + (1,) * (len(extent) - axis_at - 1))

    factor_of = one(*cuts[0])
    for cut in cuts[1:]:
        factor_of = factor_of * one(*cut)
    return factor_of


def noise(own_key, extent, scale, most, cuts=(), kind=jnp.bfloat16):
    gain = levels(own_key, extent, cuts, -0.22, 0.18) if cuts else 1.0
    entries = jax.random.normal(own_key, extent, jnp.float32) * scale * gain
    return jnp.minimum(jnp.maximum(entries, -most), most).astype(kind)


def setup_inputs(seed: int = 0, part: int = 0) -> dict:
    arg_keys = jax.random.split(jax.random.key(seed), 5)
    part_splits = jax.random.split(jax.random.fold_in(arg_keys[4], part), 5)
    psi = noise(arg_keys[0], (2, NB, NPW), 1.0, 6.0, ((1, 4), (2, 4)), jnp.float32)
    potential = jnp.clip(1.0 + 2.0 * jax.random.uniform(part_splits[1], (N, N, N), jnp.float32) ** levels(part_splits[1], (N, N, N), ((1, 4),), -0.2, 0.2), 1.0, 3.0)
    miller = draw_miller(jax.random.fold_in(arg_keys[4], 71), part)
    occupied = plant((jax.random.randint(arg_keys[3], (NB,), 0, 4) < 3).astype(jnp.int32), jax.random.fold_in(arg_keys[3], 1), 0, 1)
    return {"psi": psi, "potential": potential, "miller": miller, "occupied": occupied}


highest = lax.Precision.HIGHEST


def reference(psi, potential, miller, occupied):
    volume = N * N * N

    def apply_one(coefs):
        real_grid = jnp.zeros((volume,), coefs.dtype).at[miller].set(coefs[0])
        imag_grid = jnp.zeros((volume,), coefs.dtype).at[miller].set(coefs[1])
        field_grid = lax.complex(real_grid, imag_grid).reshape(N, N, N)
        wave_grid = jnp.fft.ifftn(field_grid) * volume
        product = wave_grid * potential
        back_grid = (jnp.fft.fftn(product) / volume).reshape(volume)[miller]
        return jnp.stack([jnp.real(back_grid), jnp.imag(back_grid)])

    applied = lax.map(apply_one, jnp.transpose(psi, (1, 0, 2)))
    applied_real = applied[:, 0]
    applied_imag = applied[:, 1]
    basis_real = psi[0]
    basis_imag = psi[1]
    over_real = jnp.dot(basis_real, applied_real.T, precision=highest) + jnp.dot(basis_imag, applied_imag.T, precision=highest)
    over_imag = jnp.dot(basis_real, applied_imag.T, precision=highest) - jnp.dot(basis_imag, applied_real.T, precision=highest)
    weights = occupied.astype(psi.dtype)[:, None]
    weight_real = weights * (over_real / NPW)
    weight_imag = weights * (over_imag / NPW)
    proj_real = jnp.dot(weight_real.T, basis_real, precision=highest) - jnp.dot(weight_imag.T, basis_imag, precision=highest)
    proj_imag = jnp.dot(weight_imag.T, basis_real, precision=highest) + jnp.dot(weight_real.T, basis_imag, precision=highest)
    return jnp.stack([applied_real - proj_real, applied_imag - proj_imag])
```

```python
import functools

import jax
import jax.numpy as jnp
import numpy as np
from jax import lax
from jax.experimental import pallas as pl
from jax.experimental.pallas import tpu as pltpu
from jax.sharding import PartitionSpec as P

F32 = jnp.float32
BF16 = jnp.bfloat16
CHUNK = 2048
ROWS = 8


def halves(value):
    high = value.astype(BF16)
    return high, (value - high.astype(F32)).astype(BF16)


def const_halves(value):
    value = np.asarray(value, np.float32)
    high = value.astype(BF16)
    return high, (value - high.astype(np.float32)).astype(BF16)


def left_const(value):
    high, low = const_halves(value)
    return jnp.asarray(np.concatenate([high, high, low], axis=1))


def right_const(value):
    high, low = const_halves(value)
    return jnp.asarray(np.concatenate([high, high, low], axis=0))


def left_mul(weights, value):
    high, low = halves(value)
    return jnp.dot(weights, jnp.concatenate([high, low, high], axis=0), preferred_element_type=F32)


def right_mul(value, weights):
    high, low = halves(value)
    return jnp.dot(jnp.concatenate([high, low, high], axis=1), weights, preferred_element_type=F32)


def turn(value, kept):
    groups = []
    for start in range(0, value.shape[1], 2 * kept):
        groups.append(-value[:, start + kept : start + 2 * kept])
        groups.append(value[:, start : start + kept])
    return jnp.concatenate(groups, axis=1)


class Sizes:
    def __init__(self, psi, potential, owners):
        self.n = potential.shape[0]
        self.owners = owners
        self.kept = self.n // 2
        self.planes = self.n // (2 * owners)
        self.inner = min(4, self.planes)
        self.outer = self.planes // self.inner
        self.block = self.n // owners
        self.points = psi.shape[2]
        self.bands = psi.shape[1]
        self.rows = self.outer * self.kept
        self.lanes = self.inner * 2 * self.kept
        self.chunk = min(CHUNK, self.points)


def twiddles(s):
    n, kept, quarter = s.n, s.kept, s.n // 4
    full = np.arange(n)
    signed = np.arange(kept) - quarter
    angle = 2.0 * np.pi / n * ((signed[:, None] * full[None, :]) % n)
    cosine, sine = np.cos(angle), np.sin(angle)
    rows_in = np.concatenate([cosine.T, sine.T], axis=1)
    rows_out = np.concatenate([cosine, -sine], axis=1) / float(n) ** 3
    z_in = np.block([[cosine, sine], [-sine, cosine]])
    z_out = np.block([[cosine.T, -sine.T], [sine.T, cosine.T]])
    inner, owner, outer = np.meshgrid(
        np.arange(s.inner), np.arange(s.owners), np.arange(s.outer), indexing="ij"
    )
    plane = ((outer * s.inner + inner) * s.owners + owner).reshape(s.inner, -1)
    cos_p, sin_p = cosine[plane], sine[plane]
    real_row = np.stack([cos_p, -sin_p], axis=1).reshape(-1, n)
    imag_row = np.stack([sin_p, cos_p], axis=1).reshape(-1, n)
    x_in = np.concatenate([real_row, imag_row], axis=1).T
    real_row = np.stack([cos_p, -sin_p], axis=1).reshape(-1, n)
    imag_row = np.stack([sin_p, cos_p], axis=1).reshape(-1, n)
    x_out = np.concatenate([real_row, imag_row], axis=1)
    return {
        "rows_in": left_const(rows_in),
        "rows_out": left_const(rows_out),
        "z_in": right_const(z_in),
        "z_out": right_const(z_out),
        "x_in": left_const(x_in),
        "x_out": left_const(x_out),
    }


def spread_kernel(s, code_ref, psi_ref, iota_ref, weight_ref, out_ref, acc):
    acc[...] = jnp.zeros_like(acc)

    @pl.loop(0, s.points // s.chunk)
    def _(step):
        at = pl.ds(pl.multiple_of(step * s.chunk, s.chunk), s.chunk)
        codes = code_ref[:, at].astype(BF16)
        high, low = halves(psi_ref[:, at])
        zero = jnp.zeros((), BF16)
        row_hot = jnp.where(iota_ref[: s.rows, :] == codes[0:1], jnp.ones((), BF16), zero)
        total = None
        for part in (high, low):
            pieces = []
            for group in range(s.inner):
                mask = iota_ref[group * s.kept : (group + 1) * s.kept, :] == codes[1:2]
                for kind in range(2):
                    pieces.append(jnp.where(mask, part[kind : kind + 1], zero))
            value = jnp.concatenate(pieces, axis=0)
            term = lax.dot_general(
                row_hot, value, (((1,), (1,)), ((), ())), preferred_element_type=F32
            )
            total = term if total is None else total + term
        acc[...] += total

    for outer in range(s.outer):
        field = acc[outer * s.kept : (outer + 1) * s.kept, :]
        both = jnp.concatenate([field, turn(field, s.kept)], axis=0)
        result = left_mul(weight_ref[...], both)
        for owner in range(s.owners):
            out_ref[owner, outer] = result[owner * s.block : (owner + 1) * s.block]


def middle_kernel(s, in_ref, pot_ref, z_in, x_in, x_out, z_out, out_ref):
    n = s.n
    gt = s.owners * s.outer
    width = 2 * s.kept
    planes = []
    for inner in range(s.inner):
        value = in_ref[:, :, inner * width : (inner + 1) * width].reshape(gt * ROWS, width)
        wide = right_mul(value, z_in[...])
        for kind in range(2):
            piece = wide[:, kind * n : (kind + 1) * n].reshape(gt, ROWS, n)
            planes.append(jnp.swapaxes(piece, 0, 1))
    columns = [
        jnp.concatenate([piece[row] for piece in planes], axis=0) for row in range(ROWS)
    ]
    wave = left_mul(x_in[...], jnp.concatenate(columns, axis=1))
    pot = jnp.swapaxes(pot_ref[...], 0, 1)
    pot = jnp.concatenate([pot[row] for row in range(ROWS)], axis=1)
    product = jnp.concatenate([wave[:n] * pot, wave[n:] * pot], axis=0)
    back = left_mul(x_out[...], product)
    for inner in range(s.inner):
        kinds = []
        for kind in range(2):
            start = (inner * 2 + kind) * gt
            piece = jnp.stack(
                [back[start : start + gt, row * n : (row + 1) * n] for row in range(ROWS)]
            )
            kinds.append(jnp.swapaxes(piece, 0, 1).reshape(gt * ROWS, n))
        narrow = right_mul(jnp.concatenate(kinds, axis=1), z_out[...])
        out_ref[:, :, inner * width : (inner + 1) * width] = narrow.reshape(gt, ROWS, width)


def pick_kernel(s, in_ref, code_ref, basis_ref, iota_ref, weight_ref, out_ref, over_ref, table):
    for outer in range(s.outer):
        rows = jnp.concatenate([in_ref[owner, outer] for owner in range(s.owners)], axis=0)
        both = jnp.concatenate([rows, turn(rows, s.kept)], axis=0)
        field = left_mul(weight_ref[...], both)
        high, low = halves(field.T)
        table[:, outer * s.kept : (outer + 1) * s.kept] = high
        table[:, s.rows + outer * s.kept : s.rows + (outer + 1) * s.kept] = low
    over_ref[...] = jnp.zeros_like(over_ref)

    @pl.loop(0, s.points // s.chunk)
    def _(step):
        at = pl.ds(pl.multiple_of(step * s.chunk, s.chunk), s.chunk)
        codes = code_ref[:, at].astype(BF16)
        one_hot = jnp.where(iota_ref[: s.rows, :] == codes[0:1], jnp.ones((), BF16), jnp.zeros((), BF16))
        found = jnp.dot(table[:, : s.rows], one_hot, preferred_element_type=F32) + jnp.dot(
            table[:, s.rows :], one_hot, preferred_element_type=F32
        )
        lane = code_ref[1:2, at]
        index = lax.broadcasted_iota(jnp.int32, (s.kept, s.chunk), 0).astype(F32)
        sums = [None, None]
        for group in range(s.inner):
            mask = index == lane - float(group * s.kept)
            for kind in range(2):
                start = (group * 2 + kind) * s.kept
                piece = jnp.where(mask, found[start : start + s.kept], 0.0)
                sums[kind] = piece if sums[kind] is None else sums[kind] + piece
        real = jnp.sum(sums[0], axis=0, keepdims=True)
        imag = jnp.sum(sums[1], axis=0, keepdims=True)
        out_ref[0:1, at] = real
        out_ref[1:2, at] = imag
        left_real = basis_ref[0, :, at]
        left_imag = basis_ref[1, :, at]
        over_ref[0] += left_real * real + left_imag * imag
        over_ref[1] += left_real * imag - left_imag * real


def local_codes(s, miller):
    quarter = s.n // 4
    points = lax.dynamic_slice_in_dim(miller, lax.axis_index("ga") * s.points, s.points)
    slot = (points // (s.n * s.n) + quarter) % s.n // s.owners
    row = (points // s.n + quarter) % s.n
    column = (points + quarter) % s.n
    high = slot // s.inner * s.kept + row
    low = slot % s.inner * s.kept + column
    return jnp.stack([high, low]).astype(F32)


VMEM = pl.BlockSpec(memory_space=pltpu.VMEM)
PARAMS = pltpu.CompilerParams(vmem_limit_bytes=56 * 1024 * 1024)


def call(kernel, s, out, count, scratch=()):
    return pl.pallas_call(
        functools.partial(kernel, s),
        out_shape=out,
        in_specs=[VMEM] * count,
        out_specs=jax.tree.map(lambda _: VMEM, out),
        scratch_shapes=list(scratch),
        compiler_params=PARAMS,
    )


def shards(psi, potential, miller, occupied):
    s = Sizes(psi, potential, lax.axis_size("ga"))
    w = twiddles(s)
    shape = jax.ShapeDtypeStruct
    basis = lax.all_gather(psi, "band", axis=1, tiled=True)
    codes = local_codes(s, miller)
    count = max(s.rows, s.inner * s.kept)
    iota = lax.broadcasted_iota(jnp.int32, (count, s.chunk), 0).astype(BF16)
    sent = call(
        spread_kernel, s, shape((s.owners, s.outer, s.block, s.lanes), F32), 4,
        [pltpu.VMEM((s.rows, s.lanes), F32)],
    )(codes, psi[:, 0], iota, w["rows_in"])
    got = lax.all_to_all(sent, "ga", split_axis=0, concat_axis=0, tiled=True)
    gt = s.owners * s.outer
    whole = [w["z_in"], w["x_in"], w["x_out"], w["z_out"]]
    sent = pl.pallas_call(
        functools.partial(middle_kernel, s),
        out_shape=shape((gt, s.block, s.lanes), F32),
        grid=(s.block // ROWS,),
        in_specs=[
            pl.BlockSpec((gt, ROWS, s.lanes), lambda i: (0, i, 0)),
            pl.BlockSpec((s.n, ROWS, s.n), lambda i: (0, i, 0)),
        ] + [pl.BlockSpec(v.shape, lambda i: (0, 0)) for v in whole],
        out_specs=pl.BlockSpec((gt, ROWS, s.lanes), lambda i: (0, i, 0)),
        compiler_params=PARAMS,
    )(got.reshape(gt, s.block, s.lanes), potential, *whole)
    sent = sent.reshape(s.owners, s.outer, s.block, s.lanes)
    got = lax.all_to_all(sent, "ga", split_axis=0, concat_axis=0, tiled=True)
    bands = basis.shape[1]
    applied, over = call(
        pick_kernel, s, (shape((2, s.points), F32), shape((2, bands, s.chunk), F32)), 5,
        [pltpu.VMEM((s.lanes, 2 * s.rows), BF16)],
    )(got, codes, basis, iota, w["rows_out"])
    total = s.points * s.owners
    over = lax.psum(jnp.sum(over, axis=2), "ga") / total * occupied.astype(F32)
    real, imag = over[0][:, None], over[1][:, None]
    proj_real = jnp.sum(basis[0] * real - basis[1] * imag, axis=0)
    proj_imag = jnp.sum(basis[0] * imag + basis[1] * real, axis=0)
    return jnp.stack([applied[0] - proj_real, applied[1] - proj_imag])[:, None]


highest = lax.Precision.HIGHEST


def phases(first_index, second_index, direction, length):
    turns = first_index[:, None] * second_index[None, :] % length
    angle = direction * 2.0 * jnp.pi / length * turns.astype(jnp.float32)
    return (jnp.cos(angle), jnp.sin(angle))


def contract(pattern, real_part, imag_part, twiddle):
    cosine, sine_part = twiddle
    out_real = jnp.einsum(pattern, real_part, cosine, precision=highest) - jnp.einsum(
        pattern, imag_part, sine_part, precision=highest
    )
    out_imag = jnp.einsum(pattern, real_part, sine_part, precision=highest) + jnp.einsum(
        pattern, imag_part, cosine, precision=highest
    )
    return (out_real, out_imag)


def inner_products(left_real, left_imag, right_real, right_imag):
    over_real = jnp.einsum("mk,nk->mn", left_real, right_real, precision=highest) + jnp.einsum(
        "mk,nk->mn", left_imag, right_imag, precision=highest
    )
    over_imag = jnp.einsum("mk,nk->mn", left_real, right_imag, precision=highest) - jnp.einsum(
        "mk,nk->mn", left_imag, right_real, precision=highest
    )
    return (over_real, over_imag)


def subtract(applied_real, applied_imag, basis_real, basis_imag, weight_real, weight_imag):
    proj_real = jnp.einsum("mn,mk->nk", weight_real, basis_real, precision=highest) - jnp.einsum(
        "mn,mk->nk", weight_imag, basis_imag, precision=highest
    )
    proj_imag = jnp.einsum("mn,mk->nk", weight_imag, basis_real, precision=highest) + jnp.einsum(
        "mn,mk->nk", weight_real, basis_imag, precision=highest
    )
    return (applied_real - proj_real, applied_imag - proj_imag)


def plain_shards(psi, potential, miller, occupied):
    grid_size = potential.shape[0]
    owners = lax.axis_size("ga")
    quarter = grid_size // 4
    per_shard = psi.shape[2]
    band_count = psi.shape[1]
    total = per_shard * lax.axis_size("ga")
    owner_index = lax.axis_index("ga")
    kept_rows = grid_size // 2
    kept_planes = grid_size // (2 * owners)
    full_index = jnp.arange(grid_size, dtype=jnp.int32)
    kept_index = (jnp.arange(kept_rows, dtype=jnp.int32) + grid_size - quarter) % grid_size
    inverse_rows = phases(kept_index, full_index, 1.0, grid_size)
    forward_rows = phases(full_index, kept_index, -1.0, grid_size)
    slot_index = jnp.arange(owners * kept_planes, dtype=jnp.int32)
    plane_index = (
        slot_index // kept_planes + owners * (slot_index % kept_planes) + grid_size - quarter
    ) % grid_size
    inverse_planes = phases(plane_index, full_index, 1.0, grid_size)
    forward_planes = phases(full_index, plane_index, -1.0, grid_size)
    local_points = lax.dynamic_slice_in_dim(miller, owner_index * per_shard, per_shard)
    index_a = local_points // (grid_size * grid_size)
    index_b = local_points // grid_size % grid_size
    index_c = local_points % grid_size
    plane_pos = (index_a + quarter) % grid_size
    position = (plane_pos // owners * kept_rows + (index_b + quarter) % grid_size) * kept_rows + (
        index_c + quarter
    ) % grid_size
    slab_size = kept_planes * kept_rows * kept_rows
    real_part = jnp.zeros((band_count, slab_size), jnp.float32).at[:, position].set(psi[0])
    imag_part = jnp.zeros((band_count, slab_size), jnp.float32).at[:, position].set(psi[1])
    real_part = real_part.reshape(band_count, kept_planes, kept_rows, kept_rows)
    imag_part = imag_part.reshape(band_count, kept_planes, kept_rows, kept_rows)
    real_part, imag_part = contract("ntbc,by->ntyc", real_part, imag_part, inverse_rows)
    pieces = (
        lax.all_to_all(real_part, "ga", split_axis=2, concat_axis=1, tiled=True),
        lax.all_to_all(imag_part, "ga", split_axis=2, concat_axis=1, tiled=True),
    )
    wide_real, wide_imag = contract("nsyc,cz->nsyz", pieces[0], pieces[1], inverse_rows)
    pieces = (wide_real, wide_imag)
    wave_real, wave_imag = contract("nsyz,sx->nxyz", pieces[0], pieces[1], inverse_planes)
    wave_real = wave_real * potential
    wave_imag = wave_imag * potential
    wide_real, wide_imag = contract("nxyz,xs->nsyz", wave_real, wave_imag, forward_planes)
    narrow = contract("nsyz,zc->nsyc", wide_real, wide_imag, forward_rows)
    real_part = lax.all_to_all(narrow[0], "ga", split_axis=1, concat_axis=2, tiled=True)
    imag_part = lax.all_to_all(narrow[1], "ga", split_axis=1, concat_axis=2, tiled=True)
    real_part, imag_part = contract("ntyc,yb->ntbc", real_part, imag_part, forward_rows)
    inverse_volume = 1.0 / grid_size**3
    applied_real = real_part.reshape(band_count, slab_size)[:, position] * inverse_volume
    applied_imag = imag_part.reshape(band_count, slab_size)[:, position] * inverse_volume
    weights = occupied.astype(jnp.float32)[:, None]
    moved_parts = (
        lax.all_to_all(applied_real, "band", split_axis=1, concat_axis=0, tiled=True),
        lax.all_to_all(applied_imag, "band", split_axis=1, concat_axis=0, tiled=True),
        lax.all_to_all(psi[0], "band", split_axis=1, concat_axis=0, tiled=True),
        lax.all_to_all(psi[1], "band", split_axis=1, concat_axis=0, tiled=True),
    )
    column_real, column_imag, basis_real, basis_imag = moved_parts
    over_real, over_imag = inner_products(basis_real, basis_imag, column_real, column_imag)
    over_real, over_imag = lax.psum((over_real, over_imag), ("ga", "band"))
    weight_real = weights * (over_real / total)
    weight_imag = weights * (over_imag / total)
    left_real, left_imag = subtract(
        column_real, column_imag, basis_real, basis_imag, weight_real, weight_imag
    )
    left_real, left_imag = (
        lax.all_to_all(left_real, "band", split_axis=0, concat_axis=1, tiled=True),
        lax.all_to_all(left_imag, "band", split_axis=0, concat_axis=1, tiled=True),
    )
    return jnp.stack([left_real, left_imag])


def solution(mesh):
    def body(psi, potential, miller, occupied):
        if potential.shape[1] % ROWS:
            return plain_shards(psi, potential, miller, occupied)
        return shards(psi, potential, miller, occupied)

    in_specs = (P(None, "band", "ga"), P("pert", "ga", None), P(), P())
    out_specs = P(None, ("pert", "band"), "ga")
    return jax.shard_map(body, mesh=mesh, in_specs=in_specs, out_specs=out_specs, check_vma=False)
```

```python
import functools

import jax
import jax.numpy as jnp
import numpy as np
from jax import lax
from jax.experimental import pallas as pl
from jax.experimental.pallas import tpu as pltpu
from jax.sharding import PartitionSpec as P

F32 = jnp.float32
BF16 = jnp.bfloat16
CHUNK = 2048
LANES = 128
MESH = pl.DeviceIdType.MESH
ROWS = 8


def halves(value):
    high = value.astype(BF16)
    return high, (value - high.astype(F32)).astype(BF16)


def const_halves(value):
    value = np.asarray(value, np.float32)
    high = value.astype(BF16)
    return high, (value - high.astype(np.float32)).astype(BF16)


def left_const(value):
    high, low = const_halves(value)
    return jnp.asarray(np.concatenate([high, high, low], axis=1))


def right_const(value):
    high, low = const_halves(value)
    return jnp.asarray(np.concatenate([high, high, low], axis=0))


def left_mul(weights, value):
    high, low = halves(value)
    return jnp.dot(weights, jnp.concatenate([high, low, high], axis=0), preferred_element_type=F32)


def right_mul(value, weights):
    high, low = halves(value)
    return jnp.dot(jnp.concatenate([high, low, high], axis=1), weights, preferred_element_type=F32)


def turn(value, kept):
    groups = []
    for start in range(0, value.shape[1], 2 * kept):
        groups.append(-value[:, start + kept : start + 2 * kept])
        groups.append(value[:, start : start + kept])
    return jnp.concatenate(groups, axis=1)


class Sizes:
    def __init__(self, psi, potential, owners):
        self.n = potential.shape[0]
        self.owners = owners
        self.kept = self.n // 2
        self.planes = self.n // (2 * owners)
        self.inner = min(4, self.planes)
        self.outer = self.planes // self.inner
        self.block = self.n // owners
        self.points = psi.shape[2]
        self.bands = psi.shape[1]
        self.rows = self.outer * self.kept
        self.lanes = self.inner * 2 * self.kept
        self.chunk = min(CHUNK, self.points)
        self.lines = self.chunk // LANES
        self.parts = 2 if self.inner % 2 == 0 else 1
        self.groups = self.inner // self.parts
        self.width = self.groups * 2 * self.kept


def twiddles(s):
    n, kept, quarter = s.n, s.kept, s.n // 4
    full = np.arange(n)
    signed = np.arange(kept) - quarter
    angle = 2.0 * np.pi / n * ((signed[:, None] * full[None, :]) % n)
    cosine, sine = np.cos(angle), np.sin(angle)
    rows_in = np.concatenate([cosine.T, sine.T], axis=1)
    rows_out = np.concatenate([cosine, -sine], axis=1) / float(n) ** 3
    z_in = np.block([[cosine, sine], [-sine, cosine]])
    z_out = np.block([[cosine.T, -sine.T], [sine.T, cosine.T]])
    inner, owner, outer = np.meshgrid(
        np.arange(s.inner), np.arange(s.owners), np.arange(s.outer), indexing="ij"
    )
    plane = ((outer * s.inner + inner) * s.owners + owner).reshape(s.inner, -1)
    cos_p, sin_p = cosine[plane], sine[plane]
    real_row = np.stack([cos_p, -sin_p], axis=1).reshape(-1, n)
    imag_row = np.stack([sin_p, cos_p], axis=1).reshape(-1, n)
    x_in = np.concatenate([real_row, imag_row], axis=1).T
    real_row = np.stack([cos_p, -sin_p], axis=1).reshape(-1, n)
    imag_row = np.stack([sin_p, cos_p], axis=1).reshape(-1, n)
    x_out = np.concatenate([real_row, imag_row], axis=1)
    return {
        "rows_in": left_const(rows_in),
        "rows_out": left_const(rows_out),
        "z_in": right_const(z_in),
        "z_out": right_const(z_out),
        "x_in": left_const(x_in),
        "x_out": left_const(x_out),
    }


def meet(axes):
    barrier = pltpu.get_barrier_semaphore()
    for axis in axes:
        size = lax.axis_size(axis)
        for step in range(1, size):
            peer = lax.rem(lax.axis_index(axis) + step, size)
            pl.semaphore_signal(barrier, inc=1, device_id={axis: peer}, device_id_type=MESH)
    pl.semaphore_wait(barrier, sum(lax.axis_size(axis) - 1 for axis in axes))


def to_peer(axis, step, source, target, send_sem, recv_sem):
    size = lax.axis_size(axis)
    peer = lax.rem(lax.axis_index(axis) + step, size)
    return pltpu.make_async_remote_copy(
        src_ref=source,
        dst_ref=target,
        send_sem=send_sem,
        recv_sem=recv_sem,
        device_id={axis: peer},
        device_id_type=MESH,
    )


def one_line(block):
    return jnp.concatenate([block[i : i + 1] for i in range(block.shape[0])], axis=1)


def fill_iota(iota_ref):
    iota_ref[...] = lax.broadcasted_iota(jnp.int32, iota_ref.shape, 0).astype(F32).astype(BF16)


def split_codes(s, packed):
    count = s.inner * s.kept
    return packed // count, packed % count


def spread_kernel(
    s, code_ref, psi_ref, weight_ref, got_ref, basis_ref,
    acc, held, iota_ref, send_sem, recv_sem, own_sem, basis_send, basis_recv,
):
    owner_at, band_at = lax.axis_index("ga"), lax.axis_index("band")
    meet(("ga", "band"))
    copies = [pltpu.make_async_copy(psi_ref, basis_ref.at[band_at], own_sem.at[s.parts])]
    for step in range(1, lax.axis_size("band")):
        copies.append(to_peer(
            "band", step, psi_ref, basis_ref.at[band_at],
            basis_send.at[step - 1], basis_recv.at[step - 1],
        ))
    for copy in copies:
        copy.start()
    fill_iota(iota_ref)
    for part in range(s.parts):
        acc[...] = jnp.zeros_like(acc)

        @pl.loop(0, s.points // s.chunk)
        def _(step):
            at = pl.ds(pl.multiple_of(step * s.lines, s.lines), s.lines)
            row_code, lane_code = split_codes(s, code_ref[at, :])
            row_code = one_line(row_code.astype(F32)).astype(BF16)
            lane_code = one_line(lane_code.astype(F32)).astype(BF16)
            values = [halves(one_line(psi_ref[kind, at, :])) for kind in range(2)]
            zero = jnp.zeros((), BF16)
            row_hot = jnp.where(iota_ref[: s.rows, :] == row_code, jnp.ones((), BF16), zero)
            masks = [
                iota_ref[group * s.kept : (group + 1) * s.kept, :] == lane_code
                for group in range(part * s.groups, (part + 1) * s.groups)
            ]
            total = None
            for half in range(2):
                value = jnp.concatenate(
                    [jnp.where(m, values[kind][half], zero) for m in masks for kind in range(2)],
                    axis=0,
                )
                term = lax.dot_general(
                    row_hot, value, (((1,), (1,)), ((), ())), preferred_element_type=F32
                )
                total = term if total is None else total + term
            acc[...] += total

        for outer in range(s.outer):
            field = acc[outer * s.kept : (outer + 1) * s.kept, :]
            both = jnp.concatenate([field, turn(field, s.kept)], axis=0)
            result = left_mul(weight_ref[...], both)
            for owner in range(s.owners):
                held[part, owner, outer] = result[owner * s.block : (owner + 1) * s.block]
        own = pltpu.make_async_copy(
            held.at[part, owner_at], got_ref.at[part, owner_at], own_sem.at[part]
        )
        own.start()
        copies.append(own)
        for step in range(1, s.owners):
            peer = lax.rem(owner_at + step, s.owners)
            copy = to_peer(
                "ga", step, held.at[part, peer], got_ref.at[part, owner_at],
                send_sem.at[part, step - 1], recv_sem.at[part, step - 1],
            )
            copy.start()
            copies.append(copy)
    for copy in copies:
        copy.wait()


def middle_kernel(
    s, in_ref, pot_ref, z_in, x_in, x_out, z_out, got_ref, held, send_sem, recv_sem, own_sem
):
    n = s.n
    gt = s.owners * s.outer
    width = 2 * s.kept
    at = pl.program_id(0)
    owner_at = lax.axis_index("ga")

    @pl.when(at == 0)
    def _():
        meet(("ga",))

    planes = []
    for inner in range(s.inner):
        part, start = inner // s.groups, inner % s.groups * width
        value = in_ref[part, :, :, start : start + width].reshape(gt * ROWS, width)
        wide = right_mul(value, z_in[...])
        for kind in range(2):
            piece = wide[:, kind * n : (kind + 1) * n].reshape(gt, ROWS, n)
            planes.append(jnp.swapaxes(piece, 0, 1))
    columns = [
        jnp.concatenate([piece[row] for piece in planes], axis=0) for row in range(ROWS)
    ]
    wave = left_mul(x_in[...], jnp.concatenate(columns, axis=1))
    pot = jnp.swapaxes(pot_ref[...], 0, 1)
    pot = jnp.concatenate([pot[row] for row in range(ROWS)], axis=1)
    product = jnp.concatenate([wave[:n] * pot, wave[n:] * pot], axis=0)
    back = left_mul(x_out[...], product)
    for inner in range(s.inner):
        kinds = []
        for kind in range(2):
            start = (inner * 2 + kind) * gt
            piece = jnp.stack(
                [back[start : start + gt, row * n : (row + 1) * n] for row in range(ROWS)]
            )
            kinds.append(jnp.swapaxes(piece, 0, 1).reshape(gt * ROWS, n))
        narrow = right_mul(jnp.concatenate(kinds, axis=1), z_out[...])
        held[at, :, :, :, inner * width : (inner + 1) * width] = narrow.reshape(
            s.owners, s.outer, ROWS, width
        )

    def copies(chunk):
        yield pltpu.make_async_copy(
            held.at[chunk, owner_at], got_ref.at[chunk, owner_at], own_sem.at[chunk]
        )
        for step in range(1, s.owners):
            peer = lax.rem(owner_at + step, s.owners)
            yield to_peer(
                "ga", step, held.at[chunk, peer], got_ref.at[chunk, owner_at],
                send_sem.at[chunk, step - 1], recv_sem.at[chunk, step - 1],
            )

    for copy in copies(at):
        copy.start()

    @pl.when(at == s.block // ROWS - 1)
    def _():
        for chunk in range(s.block // ROWS):
            for copy in copies(chunk):
                copy.wait()


def pick_kernel(
    s, in_ref, code_ref, basis_ref, occupied_ref, weight_ref, out_ref,
    table, iota_ref, sums, send_sem, recv_sem,
):
    owner_at = lax.axis_index("ga")
    bands = basis_ref.shape[0]
    meet(("ga",))
    fill_iota(iota_ref)
    for outer in range(s.outer):
        rows = jnp.concatenate(
            [
                in_ref[chunk, owner, outer]
                for owner in range(s.owners)
                for chunk in range(s.block // ROWS)
            ],
            axis=0,
        )
        both = jnp.concatenate([rows, turn(rows, s.kept)], axis=0)
        field = left_mul(weight_ref[...], both)
        high, low = halves(field.T)
        table[:, outer * s.kept : (outer + 1) * s.kept] = high
        table[:, s.rows + outer * s.kept : s.rows + (outer + 1) * s.kept] = low

    @pl.loop(0, s.points // s.chunk)
    def _(step):
        start = pl.multiple_of(step * s.lines, s.lines)
        row_code, lane_code = split_codes(s, code_ref[pl.ds(start, s.lines), :])
        row_code = one_line(row_code.astype(F32)).astype(BF16)
        lane_code = one_line(lane_code)
        one_hot = jnp.where(
            iota_ref[...] == row_code, jnp.ones((), BF16), jnp.zeros((), BF16)
        )
        found = jnp.dot(table[:, : s.rows], one_hot, preferred_element_type=F32) + jnp.dot(
            table[:, s.rows :], one_hot, preferred_element_type=F32
        )
        index = lax.broadcasted_iota(jnp.int32, (s.kept, s.chunk), 0)
        totals = [None, None]
        for group in range(s.inner):
            mask = index == lane_code - group * s.kept
            for kind in range(2):
                first = (group * 2 + kind) * s.kept
                piece = jnp.where(mask, found[first : first + s.kept], 0.0)
                totals[kind] = piece if totals[kind] is None else totals[kind] + piece
        for kind in range(2):
            line = jnp.sum(totals[kind], axis=0, keepdims=True)
            for i in range(s.lines):
                out_ref[kind, pl.ds(start + i, 1), :] = line[:, i * LANES : (i + 1) * LANES]

    real, imag = out_ref[0], out_ref[1]
    pieces = []
    for band in range(bands):
        left_real, left_imag = basis_ref[band, 0], basis_ref[band, 1]
        pieces.append(jnp.sum(left_real * real + left_imag * imag, axis=0, keepdims=True))
        pieces.append(jnp.sum(left_real * imag - left_imag * real, axis=0, keepdims=True))
    sums[owner_at] = jnp.concatenate(pieces, axis=0)
    copies = [
        to_peer(
            "ga", step, sums.at[owner_at], sums.at[owner_at],
            send_sem.at[step - 1], recv_sem.at[step - 1],
        )
        for step in range(1, s.owners)
    ]
    for copy in copies:
        copy.start()
    for copy in copies:
        copy.wait()
    total = sums[0]
    for owner in range(1, s.owners):
        total = total + sums[owner]
    total = jnp.sum(total, axis=1, keepdims=True) / float(s.points * s.owners)
    for band in range(bands):
        kept = occupied_ref[band].astype(F32)
        over_real = total[2 * band : 2 * band + 1] * kept
        over_imag = total[2 * band + 1 : 2 * band + 2] * kept
        left_real, left_imag = basis_ref[band, 0], basis_ref[band, 1]
        real = real - (left_real * over_real - left_imag * over_imag)
        imag = imag - (left_real * over_imag + left_imag * over_real)
    out_ref[0] = real
    out_ref[1] = imag


def local_codes(s, miller):
    quarter = s.n // 4
    points = lax.dynamic_slice_in_dim(miller, lax.axis_index("ga") * s.points, s.points)
    slot = (points // (s.n * s.n) + quarter) % s.n // s.owners
    row = (points // s.n + quarter) % s.n
    column = (points + quarter) % s.n
    high = slot // s.inner * s.kept + row
    low = slot % s.inner * s.kept + column
    return (high * (s.inner * s.kept) + low).reshape(-1, LANES)


VMEM = pl.BlockSpec(memory_space=pltpu.VMEM)
SMEM = pl.BlockSpec(memory_space=pltpu.SMEM)
ANY = pl.BlockSpec(memory_space=pl.ANY)
DMA = pltpu.SemaphoreType.DMA


def params(number):
    return pltpu.CompilerParams(
        vmem_limit_bytes=56 * 1024 * 1024, collective_id=number, has_side_effects=True
    )


def shards(psi, potential, miller, occupied):
    s = Sizes(psi, potential, lax.axis_size("ga"))
    w = twiddles(s)
    shape = jax.ShapeDtypeStruct
    bands = lax.axis_size("band")
    peers = s.owners - 1
    gt = s.owners * s.outer
    chunks = s.block // ROWS
    codes = local_codes(s, miller)
    dense = psi.reshape(2, s.points // LANES, LANES)
    arrived = (s.parts, s.owners, s.outer, s.block, s.width)
    got, basis = pl.pallas_call(
        functools.partial(spread_kernel, s),
        out_shape=(shape(arrived, F32), shape((bands,) + dense.shape, F32)),
        in_specs=[VMEM] * 3,
        out_specs=(ANY, ANY),
        scratch_shapes=[
            pltpu.VMEM((s.rows, s.width), F32),
            pltpu.VMEM(arrived, F32),
            pltpu.VMEM((max(s.rows, s.inner * s.kept), s.chunk), BF16),
            DMA((s.parts, peers)), DMA((s.parts, peers)), DMA((s.parts + 1,)),
            DMA((bands - 1,)), DMA((bands - 1,)),
        ],
        compiler_params=params(0),
        name="spread",
    )(codes, dense, w["rows_in"])
    whole = [w["z_in"], w["x_in"], w["x_out"], w["z_out"]]
    arrived = (chunks, s.owners, s.outer, ROWS, s.lanes)
    got = pl.pallas_call(
        functools.partial(middle_kernel, s),
        out_shape=shape(arrived, F32),
        grid=(chunks,),
        in_specs=[
            pl.BlockSpec((s.parts, gt, ROWS, s.width), lambda i: (0, 0, i, 0)),
            pl.BlockSpec((s.n, ROWS, s.n), lambda i: (0, i, 0)),
        ] + [pl.BlockSpec(v.shape, lambda i: (0, 0)) for v in whole],
        out_specs=ANY,
        scratch_shapes=[
            pltpu.VMEM(arrived, F32),
            DMA((chunks, peers)), DMA((chunks, peers)), DMA((chunks,)),
        ],
        compiler_params=params(1),
        name="middle",
    )(got.reshape(s.parts, gt, s.block, s.width), potential, *whole)
    out = pl.pallas_call(
        functools.partial(pick_kernel, s),
        out_shape=shape(dense.shape, F32),
        in_specs=[VMEM, VMEM, VMEM, SMEM, VMEM],
        out_specs=VMEM,
        scratch_shapes=[
            pltpu.VMEM((s.lanes, 2 * s.rows), BF16),
            pltpu.VMEM((s.rows, s.chunk), BF16),
            pltpu.VMEM((s.owners, 2 * bands, LANES), F32),
            DMA((peers,)), DMA((peers,)),
        ],
        compiler_params=params(2),
        name="pick",
    )(got, codes, basis, occupied, w["rows_out"])
    return out.reshape(psi.shape)


highest = lax.Precision.HIGHEST


def phases(first_index, second_index, direction, length):
    turns = first_index[:, None] * second_index[None, :] % length
    angle = direction * 2.0 * jnp.pi / length * turns.astype(jnp.float32)
    return (jnp.cos(angle), jnp.sin(angle))


def contract(pattern, real_part, imag_part, twiddle):
    cosine, sine_part = twiddle
    out_real = jnp.einsum(pattern, real_part, cosine, precision=highest) - jnp.einsum(
        pattern, imag_part, sine_part, precision=highest
    )
    out_imag = jnp.einsum(pattern, real_part, sine_part, precision=highest) + jnp.einsum(
        pattern, imag_part, cosine, precision=highest
    )
    return (out_real, out_imag)


def inner_products(left_real, left_imag, right_real, right_imag):
    over_real = jnp.einsum("mk,nk->mn", left_real, right_real, precision=highest) + jnp.einsum(
        "mk,nk->mn", left_imag, right_imag, precision=highest
    )
    over_imag = jnp.einsum("mk,nk->mn", left_real, right_imag, precision=highest) - jnp.einsum(
        "mk,nk->mn", left_imag, right_real, precision=highest
    )
    return (over_real, over_imag)


def subtract(applied_real, applied_imag, basis_real, basis_imag, weight_real, weight_imag):
    proj_real = jnp.einsum("mn,mk->nk", weight_real, basis_real, precision=highest) - jnp.einsum(
        "mn,mk->nk", weight_imag, basis_imag, precision=highest
    )
    proj_imag = jnp.einsum("mn,mk->nk", weight_imag, basis_real, precision=highest) + jnp.einsum(
        "mn,mk->nk", weight_real, basis_imag, precision=highest
    )
    return (applied_real - proj_real, applied_imag - proj_imag)


def plain_shards(psi, potential, miller, occupied):
    grid_size = potential.shape[0]
    owners = lax.axis_size("ga")
    quarter = grid_size // 4
    per_shard = psi.shape[2]
    band_count = psi.shape[1]
    total = per_shard * lax.axis_size("ga")
    owner_index = lax.axis_index("ga")
    kept_rows = grid_size // 2
    kept_planes = grid_size // (2 * owners)
    full_index = jnp.arange(grid_size, dtype=jnp.int32)
    kept_index = (jnp.arange(kept_rows, dtype=jnp.int32) + grid_size - quarter) % grid_size
    inverse_rows = phases(kept_index, full_index, 1.0, grid_size)
    forward_rows = phases(full_index, kept_index, -1.0, grid_size)
    slot_index = jnp.arange(owners * kept_planes, dtype=jnp.int32)
    plane_index = (
        slot_index // kept_planes + owners * (slot_index % kept_planes) + grid_size - quarter
    ) % grid_size
    inverse_planes = phases(plane_index, full_index, 1.0, grid_size)
    forward_planes = phases(full_index, plane_index, -1.0, grid_size)
    local_points = lax.dynamic_slice_in_dim(miller, owner_index * per_shard, per_shard)
    index_a = local_points // (grid_size * grid_size)
    index_b = local_points // grid_size % grid_size
    index_c = local_points % grid_size
    plane_pos = (index_a + quarter) % grid_size
    position = (plane_pos // owners * kept_rows + (index_b + quarter) % grid_size) * kept_rows + (
        index_c + quarter
    ) % grid_size
    slab_size = kept_planes * kept_rows * kept_rows
    real_part = jnp.zeros((band_count, slab_size), jnp.float32).at[:, position].set(psi[0])
    imag_part = jnp.zeros((band_count, slab_size), jnp.float32).at[:, position].set(psi[1])
    real_part = real_part.reshape(band_count, kept_planes, kept_rows, kept_rows)
    imag_part = imag_part.reshape(band_count, kept_planes, kept_rows, kept_rows)
    real_part, imag_part = contract("ntbc,by->ntyc", real_part, imag_part, inverse_rows)
    pieces = (
        lax.all_to_all(real_part, "ga", split_axis=2, concat_axis=1, tiled=True),
        lax.all_to_all(imag_part, "ga", split_axis=2, concat_axis=1, tiled=True),
    )
    wide_real, wide_imag = contract("nsyc,cz->nsyz", pieces[0], pieces[1], inverse_rows)
    pieces = (wide_real, wide_imag)
    wave_real, wave_imag = contract("nsyz,sx->nxyz", pieces[0], pieces[1], inverse_planes)
    wave_real = wave_real * potential
    wave_imag = wave_imag * potential
    wide_real, wide_imag = contract("nxyz,xs->nsyz", wave_real, wave_imag, forward_planes)
    narrow = contract("nsyz,zc->nsyc", wide_real, wide_imag, forward_rows)
    real_part = lax.all_to_all(narrow[0], "ga", split_axis=1, concat_axis=2, tiled=True)
    imag_part = lax.all_to_all(narrow[1], "ga", split_axis=1, concat_axis=2, tiled=True)
    real_part, imag_part = contract("ntyc,yb->ntbc", real_part, imag_part, forward_rows)
    inverse_volume = 1.0 / grid_size**3
    applied_real = real_part.reshape(band_count, slab_size)[:, position] * inverse_volume
    applied_imag = imag_part.reshape(band_count, slab_size)[:, position] * inverse_volume
    weights = occupied.astype(jnp.float32)[:, None]
    moved_parts = (
        lax.all_to_all(applied_real, "band", split_axis=1, concat_axis=0, tiled=True),
        lax.all_to_all(applied_imag, "band", split_axis=1, concat_axis=0, tiled=True),
        lax.all_to_all(psi[0], "band", split_axis=1, concat_axis=0, tiled=True),
        lax.all_to_all(psi[1], "band", split_axis=1, concat_axis=0, tiled=True),
    )
    column_real, column_imag, basis_real, basis_imag = moved_parts
    over_real, over_imag = inner_products(basis_real, basis_imag, column_real, column_imag)
    over_real, over_imag = lax.psum((over_real, over_imag), ("ga", "band"))
    weight_real = weights * (over_real / total)
    weight_imag = weights * (over_imag / total)
    left_real, left_imag = subtract(
        column_real, column_imag, basis_real, basis_imag, weight_real, weight_imag
    )
    left_real, left_imag = (
        lax.all_to_all(left_real, "band", split_axis=0, concat_axis=1, tiled=True),
        lax.all_to_all(left_imag, "band", split_axis=0, concat_axis=1, tiled=True),
    )
    return jnp.stack([left_real, left_imag])


def solution(mesh):
    def body(psi, potential, miller, occupied):
        if potential.shape[1] % ROWS:
            return plain_shards(psi, potential, miller, occupied)
        return shards(psi, potential, miller, occupied)

    in_specs = (P(None, "band", "ga"), P("pert", "ga", None), P(), P())
    out_specs = P(None, ("pert", "band"), "ga")
    return jax.shard_map(body, mesh=mesh, in_specs=in_specs, out_specs=out_specs, check_vma=False)
```

```python
import functools

import jax
import jax.numpy as jnp
import numpy as np
from jax import lax
from jax.experimental import pallas as pl
from jax.experimental.pallas import tpu as pltpu
from jax.sharding import PartitionSpec as P

F32 = jnp.float32
BF16 = jnp.bfloat16
CHUNK = 2048
LANES = 128
MESH = pl.DeviceIdType.MESH
ROWS = 8


def halves(value):
    high = value.astype(BF16)
    return high, (value - high.astype(F32)).astype(BF16)


def const_halves(value):
    value = np.asarray(value, np.float32)
    high = value.astype(BF16)
    return high, (value - high.astype(np.float32)).astype(BF16)


def left_const(value):
    high, low = const_halves(value)
    return jnp.asarray(np.concatenate([high, high, low], axis=1))


def right_const(value):
    high, low = const_halves(value)
    return jnp.asarray(np.concatenate([high, high, low], axis=0))


def left_mul(weights, value):
    high, low = halves(value)
    return jnp.dot(weights, jnp.concatenate([high, low, high], axis=0), preferred_element_type=F32)


def right_mul(value, weights):
    high, low = halves(value)
    return jnp.dot(jnp.concatenate([high, low, high], axis=1), weights, preferred_element_type=F32)


def turn(value, kept):
    groups = []
    for start in range(0, value.shape[1], 2 * kept):
        groups.append(-value[:, start + kept : start + 2 * kept])
        groups.append(value[:, start : start + kept])
    return jnp.concatenate(groups, axis=1)


class Sizes:
    def __init__(self, psi, potential, owners):
        self.n = potential.shape[0]
        self.owners = owners
        self.kept = self.n // 2
        self.planes = self.n // (2 * owners)
        self.inner = min(4, self.planes)
        self.outer = self.planes // self.inner
        self.block = self.n // owners
        self.points = psi.shape[2]
        self.bands = psi.shape[1]
        self.rows = self.outer * self.kept
        self.lanes = self.inner * 2 * self.kept
        self.chunk = min(CHUNK, self.points)
        self.lines = self.chunk // LANES
        self.parts = 2
        self.groups = self.inner // self.parts
        self.chunks = self.block // ROWS
        self.width = self.groups * 2 * self.kept


def twiddles(s):
    n, kept, quarter = s.n, s.kept, s.n // 4
    full = np.arange(n)
    signed = np.arange(kept) - quarter
    angle = 2.0 * np.pi / n * ((signed[:, None] * full[None, :]) % n)
    cosine, sine = np.cos(angle), np.sin(angle)
    rows_in = np.concatenate([cosine.T, sine.T], axis=1)
    rows_out = np.concatenate([cosine, -sine], axis=1) / float(n) ** 3
    z_in = np.block([[cosine, sine], [-sine, cosine]])
    z_out = np.block([[cosine.T, -sine.T], [sine.T, cosine.T]])
    inner, owner, outer = np.meshgrid(
        np.arange(s.inner), np.arange(s.owners), np.arange(s.outer), indexing="ij"
    )
    plane = ((outer * s.inner + inner) * s.owners + owner).reshape(s.inner, -1)
    cos_p, sin_p = cosine[plane], sine[plane]
    real_row = np.stack([cos_p, -sin_p], axis=1).reshape(-1, n)
    imag_row = np.stack([sin_p, cos_p], axis=1).reshape(-1, n)
    x_in = np.concatenate([real_row, imag_row], axis=1).T
    real_row = np.stack([cos_p, -sin_p], axis=1).reshape(-1, n)
    imag_row = np.stack([sin_p, cos_p], axis=1).reshape(-1, n)
    x_out = np.concatenate([real_row, imag_row], axis=1)
    return {
        "rows_in": left_const(rows_in),
        "rows_out": left_const(rows_out),
        "z_in": right_const(z_in),
        "z_out": right_const(z_out),
        "x_in": left_const(x_in),
        "x_out": left_const(x_out),
    }


def meet(axes):
    barrier = pltpu.get_barrier_semaphore()
    for axis in axes:
        size = lax.axis_size(axis)
        for step in range(1, size):
            peer = lax.rem(lax.axis_index(axis) + step, size)
            pl.semaphore_signal(barrier, inc=1, device_id={axis: peer}, device_id_type=MESH)
    pl.semaphore_wait(barrier, sum(lax.axis_size(axis) - 1 for axis in axes))


def to_peer(axis, step, source, target, send_sem, recv_sem):
    size = lax.axis_size(axis)
    peer = lax.rem(lax.axis_index(axis) + step, size)
    return pltpu.make_async_remote_copy(
        src_ref=source,
        dst_ref=target,
        send_sem=send_sem,
        recv_sem=recv_sem,
        device_id={axis: peer},
        device_id_type=MESH,
    )


def one_line(block):
    return jnp.concatenate([block[i : i + 1] for i in range(block.shape[0])], axis=1)


def fill_iota(iota_ref):
    iota_ref[...] = lax.broadcasted_iota(jnp.int32, iota_ref.shape, 0).astype(F32).astype(BF16)


def log2(value):
    return value.bit_length() - 1


def find_codes(s, points):
    n, quarter = s.n, s.n // 4
    plane = lax.shift_right_logical(points, 2 * log2(n)) + quarter & n - 1
    slot = lax.shift_right_logical(plane, log2(s.owners))
    row = lax.shift_right_logical(points, log2(n)) + quarter & n - 1
    column = points + quarter & n - 1
    outer = lax.shift_right_logical(slot, log2(s.inner))
    return outer * s.kept + row, (slot & s.inner - 1) * s.kept + column


def scatter(s, part, codes, psi_ref, iota_ref, acc):
    acc[...] = jnp.zeros_like(acc)

    @pl.loop(0, s.points // s.chunk)
    def _(step):
        at = pl.ds(pl.multiple_of(step * s.lines, s.lines), s.lines)
        row_code = one_line(codes[0, at, :].astype(F32)).astype(BF16)
        lane_code = codes[1, at, :] - part * (s.groups * s.kept)
        lane_code = one_line(lane_code.astype(F32)).astype(BF16)
        values = [halves(one_line(psi_ref[kind, at, :])) for kind in range(2)]
        zero = jnp.zeros((), BF16)
        row_hot = jnp.where(iota_ref[: s.rows, :] == row_code, jnp.ones((), BF16), zero)
        masks = [
            iota_ref[group * s.kept : (group + 1) * s.kept, :] == lane_code
            for group in range(s.groups)
        ]
        total = None
        for half in range(2):
            value = jnp.concatenate(
                [jnp.where(m, values[kind][half], zero) for m in masks for kind in range(2)],
                axis=0,
            )
            term = lax.dot_general(
                row_hot, value, (((1,), (1,)), ((), ())), preferred_element_type=F32
            )
            total = term if total is None else total + term
        acc[...] += total


def apply_rows(s, at, landed, pot_vmem, weights, held):
    z_in, x_in, x_out, z_out = weights
    n = s.n
    gt = s.owners * s.outer
    width = 2 * s.kept
    rows_at = pl.ds(pl.multiple_of(at * ROWS, ROWS), ROWS)
    planes = []
    for inner in range(s.inner):
        part, start = inner // s.groups, inner % s.groups * width
        value = landed[part, :, :, rows_at, start : start + width].reshape(gt * ROWS, width)
        wide = right_mul(value, z_in[...])
        for kind in range(2):
            piece = wide[:, kind * n : (kind + 1) * n].reshape(gt, ROWS, n)
            planes.append(jnp.swapaxes(piece, 0, 1))
    columns = [
        jnp.concatenate([piece[row] for piece in planes], axis=0) for row in range(ROWS)
    ]
    wave = left_mul(x_in[...], jnp.concatenate(columns, axis=1))
    pot = jnp.swapaxes(pot_vmem[:, rows_at, :], 0, 1)
    pot = jnp.concatenate([pot[row] for row in range(ROWS)], axis=1)
    product = jnp.concatenate([wave[:n] * pot, wave[n:] * pot], axis=0)
    back = left_mul(x_out[...], product)
    for inner in range(s.inner):
        part, first = inner // s.groups, inner % s.groups * width
        kinds = []
        for kind in range(2):
            start = (inner * 2 + kind) * gt
            piece = jnp.stack(
                [back[start : start + gt, row * n : (row + 1) * n] for row in range(ROWS)]
            )
            kinds.append(jnp.swapaxes(piece, 0, 1).reshape(gt * ROWS, n))
        narrow = right_mul(jnp.concatenate(kinds, axis=1), z_out[...])
        held[part, :, at, :, :, first : first + width] = narrow.reshape(
            s.owners, s.outer, ROWS, width
        )


def gather(s, part, codes, iota_ref, table, out_ref):
    @pl.loop(0, s.points // s.chunk)
    def _(step):
        start = pl.multiple_of(step * s.lines, s.lines)
        at = pl.ds(start, s.lines)
        row_code = one_line(codes[0, at, :].astype(F32)).astype(BF16)
        lane_code = one_line(codes[1, at, :])
        one_hot = jnp.where(
            iota_ref[: s.rows, :] == row_code, jnp.ones((), BF16), jnp.zeros((), BF16)
        )
        found = jnp.dot(
            table[...], jnp.concatenate([one_hot, one_hot], axis=0), preferred_element_type=F32
        )
        index = lax.broadcasted_iota(jnp.int32, (s.kept, s.chunk), 0)
        totals = [None, None]
        for group in range(s.groups):
            mask = index == lane_code - (part * s.groups + group) * s.kept
            for kind in range(2):
                first = (group * 2 + kind) * s.kept
                piece = jnp.where(mask, found[first : first + s.kept], 0.0)
                totals[kind] = piece if totals[kind] is None else totals[kind] + piece
        for kind in range(2):
            line = jnp.sum(totals[kind], axis=0, keepdims=True)
            for i in range(s.lines):
                value = line[:, i * LANES : (i + 1) * LANES]
                if part:
                    value = value + out_ref[kind, pl.ds(start + i, 1), :]
                out_ref[kind, pl.ds(start + i, 1), :] = value


def whole_kernel(
    s, miller_ref, psi_ref, pot_ref, occupied_ref,
    rows_in, z_in, x_in, x_out, z_out, rows_out, out_ref,
    points, codes, basis, pot_vmem, iota_ref, acc, held, landed, back_held, back_landed,
    table, sums, local_sem, basis_send, basis_recv, send_sem, recv_sem, swap_send, swap_recv,
    first_send, first_recv, first_own, back_send, back_recv, back_own, sum_send, sum_recv,
):
    owner_at, band_at = lax.axis_index("ga"), lax.axis_index("band")
    part_at = lax.axis_index("pert")
    lines = s.points // LANES
    bands = basis.shape[0]
    sources = [lax.rem(owner_at + s.owners - step, s.owners) for step in range(s.owners)]
    targets = [lax.rem(owner_at + step, s.owners) for step in range(s.owners)]
    find = pltpu.make_async_copy(
        miller_ref.at[pl.ds(pl.multiple_of(owner_at * lines, lines), lines), :],
        points, local_sem.at[0],
    )
    find.start()
    fetch = pltpu.make_async_copy(pot_ref, pot_vmem, local_sem.at[1])
    fetch.start()
    keep = pltpu.make_async_copy(psi_ref, basis.at[band_at], local_sem.at[2])
    keep.start()
    meet(("ga", "band", "pert"))
    spread = [
        to_peer(
            "band", step, psi_ref, basis.at[band_at],
            basis_send.at[step - 1], basis_recv.at[step - 1],
        )
        for step in range(1, bands)
    ]
    for copy in spread:
        copy.start()
    fill_iota(iota_ref)
    find.wait()
    row_code, lane_code = find_codes(s, points[...])
    codes[0] = row_code
    codes[1] = lane_code
    scatter(s, part_at, codes, psi_ref, iota_ref, acc)
    for outer in range(s.outer):
        field = acc[outer * s.kept : (outer + 1) * s.kept, :]
        both = jnp.concatenate([field, turn(field, s.kept)], axis=0)
        result = left_mul(rows_in[...], both)
        for owner in range(s.owners):
            held[owner, outer] = result[owner * s.block : (owner + 1) * s.block]
    out = [
        to_peer(
            "ga", step, held.at[targets[step]], landed.at[part_at, owner_at],
            send_sem.at[step - 1], recv_sem.at[step - 1],
        )
        for step in range(1, s.owners)
    ]
    for copy in out:
        copy.start()
    own = pltpu.make_async_copy(held.at[owner_at], landed.at[part_at, owner_at], local_sem.at[3])
    own.start()
    swaps = []
    for step in range(s.owners):
        if step:
            out[step - 1].wait_recv()
            source = landed.at[part_at, sources[step]]
        else:
            source = held.at[owner_at]
        swap = to_peer(
            "pert", 1, source, landed.at[part_at, sources[step]],
            swap_send.at[step], swap_recv.at[step],
        )
        swap.start()
        swaps.append(swap)
    fetch.wait()
    own.wait()
    for swap in swaps:
        swap.wait_recv()

    weights = (z_in, x_in, x_out, z_out)

    def early(at, step):
        return to_peer(
            "ga", step, back_held.at[0, targets[step], at], back_landed.at[0, owner_at, at],
            first_send.at[at, step - 1], first_recv.at[at, step - 1],
        )

    @pl.loop(0, s.chunks)
    def _(at):
        apply_rows(s, at, landed, pot_vmem, weights, back_held)
        for step in range(1, s.owners):
            early(at, step).start()

    late = [
        to_peer(
            "ga", step, back_held.at[1, targets[step]], back_landed.at[1, owner_at],
            back_send.at[step - 1], back_recv.at[step - 1],
        )
        for step in range(1, s.owners)
    ]
    for copy in late:
        copy.start()
    mine = [
        pltpu.make_async_copy(
            back_held.at[part, owner_at], back_landed.at[part, owner_at], back_own.at[part]
        )
        for part in range(s.parts)
    ]
    for copy in mine:
        copy.start()
    for part in range(s.parts):
        mine[part].wait()
        if part == 0:
            for at in range(s.chunks):
                for step in range(1, s.owners):
                    early(at, step).wait_recv()
        else:
            for copy in late:
                copy.wait_recv()
        for outer in range(s.outer):
            rows = jnp.concatenate(
                [
                    back_landed[part, owner, at, outer]
                    for owner in range(s.owners)
                    for at in range(s.chunks)
                ],
                axis=0,
            )
            both = jnp.concatenate([rows, turn(rows, s.kept)], axis=0)
            high, low = halves(left_mul(rows_out[...], both).T)
            table[:, outer * s.kept : (outer + 1) * s.kept] = high
            table[:, s.rows + outer * s.kept : s.rows + (outer + 1) * s.kept] = low
        gather(s, part, codes, iota_ref, table, out_ref)

    keep.wait()
    for copy in spread:
        copy.wait_recv()
    real, imag = out_ref[0], out_ref[1]
    pieces = []
    for band in range(bands):
        left_real, left_imag = basis[band, 0], basis[band, 1]
        pieces.append(jnp.sum(left_real * real + left_imag * imag, axis=0, keepdims=True))
        pieces.append(jnp.sum(left_real * imag - left_imag * real, axis=0, keepdims=True))
    sums[owner_at] = jnp.concatenate(pieces, axis=0)
    adds = [
        to_peer(
            "ga", step, sums.at[owner_at], sums.at[owner_at],
            sum_send.at[step - 1], sum_recv.at[step - 1],
        )
        for step in range(1, s.owners)
    ]
    for copy in adds:
        copy.start()
    for copy in adds:
        copy.wait_recv()
    total = sums[0]
    for owner in range(1, s.owners):
        total = total + sums[owner]
    total = jnp.sum(total, axis=1, keepdims=True) / float(s.points * s.owners)
    for band in range(bands):
        kept = occupied_ref[band].astype(F32)
        over_real = total[2 * band : 2 * band + 1] * kept
        over_imag = total[2 * band + 1 : 2 * band + 2] * kept
        left_real, left_imag = basis[band, 0], basis[band, 1]
        real = real - (left_real * over_real - left_imag * over_imag)
        imag = imag - (left_real * over_imag + left_imag * over_real)
    out_ref[0] = real
    out_ref[1] = imag
    for at in range(s.chunks):
        for step in range(1, s.owners):
            early(at, step).wait_send()
    for copy in spread + out + swaps + late + adds:
        copy.wait_send()


VMEM = pl.BlockSpec(memory_space=pltpu.VMEM)
SMEM = pl.BlockSpec(memory_space=pltpu.SMEM)
ANY = pl.BlockSpec(memory_space=pl.ANY)
DMA = pltpu.SemaphoreType.DMA


def shards(psi, potential, miller, occupied):
    s = Sizes(psi, potential, lax.axis_size("ga"))
    w = twiddles(s)
    bands = lax.axis_size("band")
    peers = s.owners - 1
    lines = s.points // LANES
    dense = (2, lines, LANES)
    names = ("rows_in", "z_in", "x_in", "x_out", "z_out", "rows_out")
    back = (s.parts, s.owners, s.chunks, s.outer, ROWS, s.width)
    out = pl.pallas_call(
        functools.partial(whole_kernel, s),
        out_shape=jax.ShapeDtypeStruct(dense, F32),
        in_specs=[ANY, VMEM, ANY, SMEM] + [VMEM] * len(names),
        out_specs=VMEM,
        scratch_shapes=[
            pltpu.VMEM((lines, LANES), jnp.int32),
            pltpu.VMEM(dense, jnp.int32),
            pltpu.VMEM((bands,) + dense, F32),
            pltpu.VMEM(potential.shape, F32),
            pltpu.VMEM((max(s.rows, s.groups * s.kept), s.chunk), BF16),
            pltpu.VMEM((s.rows, s.width), F32),
            pltpu.VMEM((s.owners, s.outer, s.block, s.width), F32),
            pltpu.VMEM((s.parts, s.owners, s.outer, s.block, s.width), F32),
            pltpu.VMEM(back, F32),
            pltpu.VMEM(back, F32),
            pltpu.VMEM((s.width, 2 * s.rows), BF16),
            pltpu.VMEM((s.owners, 2 * bands, LANES), F32),
            DMA((4,)),
            DMA((bands - 1,)), DMA((bands - 1,)),
            DMA((peers,)), DMA((peers,)),
            DMA((s.owners,)), DMA((s.owners,)),
            DMA((s.chunks, peers)), DMA((s.chunks, peers)), DMA((s.chunks,)),
            DMA((peers,)), DMA((peers,)), DMA((s.parts,)),
            DMA((peers,)), DMA((peers,)),
        ],
        compiler_params=pltpu.CompilerParams(
            vmem_limit_bytes=56 * 1024 * 1024, collective_id=0, has_side_effects=True
        ),
        name="whole",
    )(
        miller.reshape(-1, LANES), psi.reshape(dense), potential, occupied,
        *[w[name] for name in names],
    )
    return out.reshape(psi.shape)


highest = lax.Precision.HIGHEST


def phases(first_index, second_index, direction, length):
    turns = first_index[:, None] * second_index[None, :] % length
    angle = direction * 2.0 * jnp.pi / length * turns.astype(jnp.float32)
    return (jnp.cos(angle), jnp.sin(angle))


def contract(pattern, real_part, imag_part, twiddle):
    cosine, sine_part = twiddle
    out_real = jnp.einsum(pattern, real_part, cosine, precision=highest) - jnp.einsum(
        pattern, imag_part, sine_part, precision=highest
    )
    out_imag = jnp.einsum(pattern, real_part, sine_part, precision=highest) + jnp.einsum(
        pattern, imag_part, cosine, precision=highest
    )
    return (out_real, out_imag)


def inner_products(left_real, left_imag, right_real, right_imag):
    over_real = jnp.einsum("mk,nk->mn", left_real, right_real, precision=highest) + jnp.einsum(
        "mk,nk->mn", left_imag, right_imag, precision=highest
    )
    over_imag = jnp.einsum("mk,nk->mn", left_real, right_imag, precision=highest) - jnp.einsum(
        "mk,nk->mn", left_imag, right_real, precision=highest
    )
    return (over_real, over_imag)


def subtract(applied_real, applied_imag, basis_real, basis_imag, weight_real, weight_imag):
    proj_real = jnp.einsum("mn,mk->nk", weight_real, basis_real, precision=highest) - jnp.einsum(
        "mn,mk->nk", weight_imag, basis_imag, precision=highest
    )
    proj_imag = jnp.einsum("mn,mk->nk", weight_imag, basis_real, precision=highest) + jnp.einsum(
        "mn,mk->nk", weight_real, basis_imag, precision=highest
    )
    return (applied_real - proj_real, applied_imag - proj_imag)


def plain_shards(psi, potential, miller, occupied):
    grid_size = potential.shape[0]
    owners = lax.axis_size("ga")
    quarter = grid_size // 4
    per_shard = psi.shape[2]
    band_count = psi.shape[1]
    total = per_shard * lax.axis_size("ga")
    owner_index = lax.axis_index("ga")
    kept_rows = grid_size // 2
    kept_planes = grid_size // (2 * owners)
    full_index = jnp.arange(grid_size, dtype=jnp.int32)
    kept_index = (jnp.arange(kept_rows, dtype=jnp.int32) + grid_size - quarter) % grid_size
    inverse_rows = phases(kept_index, full_index, 1.0, grid_size)
    forward_rows = phases(full_index, kept_index, -1.0, grid_size)
    slot_index = jnp.arange(owners * kept_planes, dtype=jnp.int32)
    plane_index = (
        slot_index // kept_planes + owners * (slot_index % kept_planes) + grid_size - quarter
    ) % grid_size
    inverse_planes = phases(plane_index, full_index, 1.0, grid_size)
    forward_planes = phases(full_index, plane_index, -1.0, grid_size)
    local_points = lax.dynamic_slice_in_dim(miller, owner_index * per_shard, per_shard)
    index_a = local_points // (grid_size * grid_size)
    index_b = local_points // grid_size % grid_size
    index_c = local_points % grid_size
    plane_pos = (index_a + quarter) % grid_size
    position = (plane_pos // owners * kept_rows + (index_b + quarter) % grid_size) * kept_rows + (
        index_c + quarter
    ) % grid_size
    slab_size = kept_planes * kept_rows * kept_rows
    real_part = jnp.zeros((band_count, slab_size), jnp.float32).at[:, position].set(psi[0])
    imag_part = jnp.zeros((band_count, slab_size), jnp.float32).at[:, position].set(psi[1])
    real_part = real_part.reshape(band_count, kept_planes, kept_rows, kept_rows)
    imag_part = imag_part.reshape(band_count, kept_planes, kept_rows, kept_rows)
    real_part, imag_part = contract("ntbc,by->ntyc", real_part, imag_part, inverse_rows)
    pieces = (
        lax.all_to_all(real_part, "ga", split_axis=2, concat_axis=1, tiled=True),
        lax.all_to_all(imag_part, "ga", split_axis=2, concat_axis=1, tiled=True),
    )
    wide_real, wide_imag = contract("nsyc,cz->nsyz", pieces[0], pieces[1], inverse_rows)
    pieces = (wide_real, wide_imag)
    wave_real, wave_imag = contract("nsyz,sx->nxyz", pieces[0], pieces[1], inverse_planes)
    wave_real = wave_real * potential
    wave_imag = wave_imag * potential
    wide_real, wide_imag = contract("nxyz,xs->nsyz", wave_real, wave_imag, forward_planes)
    narrow = contract("nsyz,zc->nsyc", wide_real, wide_imag, forward_rows)
    real_part = lax.all_to_all(narrow[0], "ga", split_axis=1, concat_axis=2, tiled=True)
    imag_part = lax.all_to_all(narrow[1], "ga", split_axis=1, concat_axis=2, tiled=True)
    real_part, imag_part = contract("ntyc,yb->ntbc", real_part, imag_part, forward_rows)
    inverse_volume = 1.0 / grid_size**3
    applied_real = real_part.reshape(band_count, slab_size)[:, position] * inverse_volume
    applied_imag = imag_part.reshape(band_count, slab_size)[:, position] * inverse_volume
    weights = occupied.astype(jnp.float32)[:, None]
    moved_parts = (
        lax.all_to_all(applied_real, "band", split_axis=1, concat_axis=0, tiled=True),
        lax.all_to_all(applied_imag, "band", split_axis=1, concat_axis=0, tiled=True),
        lax.all_to_all(psi[0], "band", split_axis=1, concat_axis=0, tiled=True),
        lax.all_to_all(psi[1], "band", split_axis=1, concat_axis=0, tiled=True),
    )
    column_real, column_imag, basis_real, basis_imag = moved_parts
    over_real, over_imag = inner_products(basis_real, basis_imag, column_real, column_imag)
    over_real, over_imag = lax.psum((over_real, over_imag), ("ga", "band"))
    weight_real = weights * (over_real / total)
    weight_imag = weights * (over_imag / total)
    left_real, left_imag = subtract(
        column_real, column_imag, basis_real, basis_imag, weight_real, weight_imag
    )
    left_real, left_imag = (
        lax.all_to_all(left_real, "band", split_axis=0, concat_axis=1, tiled=True),
        lax.all_to_all(left_imag, "band", split_axis=0, concat_axis=1, tiled=True),
    )
    return jnp.stack([left_real, left_imag])


def solution(mesh):
    def body(psi, potential, miller, occupied):
        if potential.shape[1] % ROWS or lax.axis_size("pert") != 2:
            return plain_shards(psi, potential, miller, occupied)
        return shards(psi, potential, miller, occupied)

    in_specs = (P(None, "band", "ga"), P("pert", "ga", None), P(), P())
    out_specs = P(None, ("pert", "band"), "ga")
    return jax.shard_map(body, mesh=mesh, in_specs=in_specs, out_specs=out_specs, check_vma=False)
```

```python
import functools

import jax
import jax.numpy as jnp
import numpy as np
from jax import lax
from jax.experimental import pallas as pl
from jax.experimental.pallas import tpu as pltpu
from jax.sharding import PartitionSpec as P

F32 = jnp.float32
BF16 = jnp.bfloat16
CHUNK = 8192
LANES = 128
MESH = pl.DeviceIdType.MESH
ROWS = 8


def halves(value):
    high = value.astype(BF16)
    return high, (value - high.astype(F32)).astype(BF16)


def const_halves(value):
    value = np.asarray(value, np.float32)
    high = value.astype(BF16)
    return high, (value - high.astype(np.float32)).astype(BF16)


def left_const(value):
    high, low = const_halves(value)
    return jnp.asarray(np.concatenate([high, high, low], axis=1))


def right_const(value):
    high, low = const_halves(value)
    return jnp.asarray(np.concatenate([high, high, low], axis=0))


def left_mul(weights, value):
    high, low = halves(value)
    return jnp.dot(weights, jnp.concatenate([high, low, high], axis=0), preferred_element_type=F32)


def right_mul(value, weights):
    high, low = halves(value)
    return jnp.dot(jnp.concatenate([high, low, high], axis=1), weights, preferred_element_type=F32)


def turn(value, kept):
    groups = []
    for start in range(0, value.shape[1], 2 * kept):
        groups.append(-value[:, start + kept : start + 2 * kept])
        groups.append(value[:, start : start + kept])
    return jnp.concatenate(groups, axis=1)


class Sizes:
    def __init__(self, psi, potential, owners):
        self.n = potential.shape[0]
        self.owners = owners
        self.kept = self.n // 2
        self.planes = self.n // (2 * owners)
        self.inner = min(4, self.planes)
        self.outer = self.planes // self.inner
        self.block = self.n // owners
        self.points = psi.shape[2]
        self.bands = psi.shape[1]
        self.rows = self.outer * self.kept
        self.lanes = self.inner * 2 * self.kept
        self.chunk = min(CHUNK, self.points)
        self.lines = self.chunk // LANES
        self.parts = 2
        self.groups = self.inner // self.parts
        self.chunks = self.block // ROWS
        self.width = self.groups * 2 * self.kept


def twiddles(s):
    n, kept, quarter = s.n, s.kept, s.n // 4
    full = np.arange(n)
    signed = np.arange(kept) - quarter
    angle = 2.0 * np.pi / n * ((signed[:, None] * full[None, :]) % n)
    cosine, sine = np.cos(angle), np.sin(angle)
    rows_in = np.concatenate([cosine.T, sine.T], axis=1)
    rows_out = np.concatenate([cosine, -sine], axis=1) / float(n) ** 3
    z_in = np.block([[cosine, sine], [-sine, cosine]])
    z_out = np.block([[cosine.T, -sine.T], [sine.T, cosine.T]])
    inner, owner, outer = np.meshgrid(
        np.arange(s.inner), np.arange(s.owners), np.arange(s.outer), indexing="ij"
    )
    plane = ((outer * s.inner + inner) * s.owners + owner).reshape(s.inner, -1)
    cos_p, sin_p = cosine[plane], sine[plane]
    real_row = np.stack([cos_p, -sin_p], axis=1).reshape(-1, n)
    imag_row = np.stack([sin_p, cos_p], axis=1).reshape(-1, n)
    x_in = np.concatenate([real_row, imag_row], axis=1).T
    real_row = np.stack([cos_p, -sin_p], axis=1).reshape(-1, n)
    imag_row = np.stack([sin_p, cos_p], axis=1).reshape(-1, n)
    x_out = np.concatenate([real_row, imag_row], axis=1)
    return {
        "rows_in": left_const(rows_in),
        "rows_out": left_const(rows_out),
        "z_in": right_const(z_in),
        "z_out": right_const(z_out),
        "x_in": left_const(x_in),
        "x_out": left_const(x_out),
    }


def meet(axes):
    barrier = pltpu.get_barrier_semaphore()
    for axis in axes:
        size = lax.axis_size(axis)
        for step in range(1, size):
            peer = lax.rem(lax.axis_index(axis) + step, size)
            pl.semaphore_signal(barrier, inc=1, device_id={axis: peer}, device_id_type=MESH)
    pl.semaphore_wait(barrier, sum(lax.axis_size(axis) - 1 for axis in axes))


def to_peer(axis, step, source, target, send_sem, recv_sem):
    size = lax.axis_size(axis)
    peer = lax.rem(lax.axis_index(axis) + step, size)
    return pltpu.make_async_remote_copy(
        src_ref=source,
        dst_ref=target,
        send_sem=send_sem,
        recv_sem=recv_sem,
        device_id={axis: peer},
        device_id_type=MESH,
    )


def one_line(block):
    return jnp.concatenate([block[i : i + 1] for i in range(block.shape[0])], axis=1)


def fill_iota(iota_ref):
    iota_ref[...] = lax.broadcasted_iota(jnp.int32, iota_ref.shape, 0).astype(F32).astype(BF16)


def log2(value):
    return value.bit_length() - 1


def find_codes(s, points):
    n, quarter = s.n, s.n // 4
    plane = lax.shift_right_logical(points, 2 * log2(n)) + quarter & n - 1
    slot = lax.shift_right_logical(plane, log2(s.owners))
    row = lax.shift_right_logical(points, log2(n)) + quarter & n - 1
    column = points + quarter & n - 1
    outer = lax.shift_right_logical(slot, log2(s.inner))
    return outer * s.kept + row, (slot & s.inner - 1) * s.kept + column


def scatter(s, part, codes, psi_ref, iota_ref, acc):
    acc[...] = jnp.zeros_like(acc)

    @pl.loop(0, s.points // s.chunk)
    def _(step):
        at = pl.ds(pl.multiple_of(step * s.lines, s.lines), s.lines)
        row_code = one_line(codes[0, at, :].astype(F32)).astype(BF16)
        lane_code = codes[1, at, :] - part * (s.groups * s.kept)
        lane_code = one_line(lane_code.astype(F32)).astype(BF16)
        values = [halves(one_line(psi_ref[kind, at, :])) for kind in range(2)]
        zero = jnp.zeros((), BF16)
        row_hot = jnp.where(iota_ref[: s.rows, :] == row_code, jnp.ones((), BF16), zero)
        masks = [
            iota_ref[group * s.kept : (group + 1) * s.kept, :] == lane_code
            for group in range(s.groups)
        ]
        total = None
        for half in range(2):
            value = jnp.concatenate(
                [jnp.where(m, values[kind][half], zero) for m in masks for kind in range(2)],
                axis=0,
            )
            term = lax.dot_general(
                row_hot, value, (((1,), (1,)), ((), ())), preferred_element_type=F32
            )
            total = term if total is None else total + term
        acc[...] += total


def apply_rows(s, at, landed, pot_vmem, weights, held):
    z_in, x_in, x_out, z_out = weights
    n = s.n
    gt = s.owners * s.outer
    width = 2 * s.kept
    rows_at = pl.ds(pl.multiple_of(at * ROWS, ROWS), ROWS)
    planes = []
    for inner in range(s.inner):
        part, start = inner // s.groups, inner % s.groups * width
        value = landed[part, :, :, rows_at, start : start + width].reshape(gt * ROWS, width)
        wide = right_mul(value, z_in[...])
        for kind in range(2):
            piece = wide[:, kind * n : (kind + 1) * n].reshape(gt, ROWS, n)
            planes.append(jnp.swapaxes(piece, 0, 1))
    columns = [
        jnp.concatenate([piece[row] for piece in planes], axis=0) for row in range(ROWS)
    ]
    wave = left_mul(x_in[...], jnp.concatenate(columns, axis=1))
    pot = jnp.swapaxes(pot_vmem[:, rows_at, :], 0, 1)
    pot = jnp.concatenate([pot[row] for row in range(ROWS)], axis=1)
    product = jnp.concatenate([wave[:n] * pot, wave[n:] * pot], axis=0)
    back = left_mul(x_out[...], product)
    for inner in range(s.inner):
        part, first = inner // s.groups, inner % s.groups * width
        kinds = []
        for kind in range(2):
            start = (inner * 2 + kind) * gt
            piece = jnp.stack(
                [back[start : start + gt, row * n : (row + 1) * n] for row in range(ROWS)]
            )
            kinds.append(jnp.swapaxes(piece, 0, 1).reshape(gt * ROWS, n))
        narrow = right_mul(jnp.concatenate(kinds, axis=1), z_out[...])
        held[part, :, at, :, :, first : first + width] = narrow.reshape(
            s.owners, s.outer, ROWS, width
        )


def gather(s, part, codes, iota_ref, table, out_ref):
    @pl.loop(0, s.points // s.chunk)
    def _(step):
        start = pl.multiple_of(step * s.lines, s.lines)
        at = pl.ds(start, s.lines)
        row_code = one_line(codes[0, at, :].astype(F32)).astype(BF16)
        lane_code = one_line(codes[1, at, :])
        one_hot = jnp.where(
            iota_ref[: s.rows, :] == row_code, jnp.ones((), BF16), jnp.zeros((), BF16)
        )
        found = jnp.dot(
            table[...], jnp.concatenate([one_hot, one_hot], axis=0), preferred_element_type=F32
        )
        index = lax.broadcasted_iota(jnp.int32, (s.kept, s.chunk), 0)
        totals = [None, None]
        for group in range(s.groups):
            mask = index == lane_code - (part * s.groups + group) * s.kept
            for kind in range(2):
                first = (group * 2 + kind) * s.kept
                piece = jnp.where(mask, found[first : first + s.kept], 0.0)
                totals[kind] = piece if totals[kind] is None else totals[kind] + piece
        for kind in range(2):
            line = jnp.sum(totals[kind], axis=0, keepdims=True)
            for i in range(s.lines):
                value = line[:, i * LANES : (i + 1) * LANES]
                if part:
                    value = value + out_ref[kind, pl.ds(start + i, 1), :]
                out_ref[kind, pl.ds(start + i, 1), :] = value


def whole_kernel(
    s, miller_ref, psi_ref, pot_ref, occupied_ref,
    rows_in, z_in, x_in, x_out, z_out, rows_out, out_ref,
    points, codes, basis, pot_vmem, iota_ref, acc, held, landed, back_held, back_landed,
    table, sums, local_sem, basis_send, basis_recv, send_sem, recv_sem, swap_send, swap_recv,
    first_send, first_recv, first_own, back_send, back_recv, back_own, sum_send, sum_recv,
):
    owner_at, band_at = lax.axis_index("ga"), lax.axis_index("band")
    part_at = lax.axis_index("pert")
    lines = s.points // LANES
    bands = basis.shape[0]
    sources = [lax.rem(owner_at + s.owners - step, s.owners) for step in range(s.owners)]
    targets = [lax.rem(owner_at + step, s.owners) for step in range(s.owners)]
    find = pltpu.make_async_copy(
        miller_ref.at[pl.ds(pl.multiple_of(owner_at * lines, lines), lines), :],
        points, local_sem.at[0],
    )
    find.start()
    fetch = pltpu.make_async_copy(pot_ref, pot_vmem, local_sem.at[1])
    fetch.start()
    keep = pltpu.make_async_copy(psi_ref, basis.at[band_at], local_sem.at[2])
    keep.start()
    meet(("ga", "band", "pert"))
    spread = [
        to_peer(
            "band", step, psi_ref, basis.at[band_at],
            basis_send.at[step - 1], basis_recv.at[step - 1],
        )
        for step in range(1, bands)
    ]
    for copy in spread:
        copy.start()
    fill_iota(iota_ref)
    find.wait()
    row_code, lane_code = find_codes(s, points[...])
    codes[0] = row_code
    codes[1] = lane_code
    scatter(s, part_at, codes, psi_ref, iota_ref, acc)
    for outer in range(s.outer):
        field = acc[outer * s.kept : (outer + 1) * s.kept, :]
        both = jnp.concatenate([field, turn(field, s.kept)], axis=0)
        result = left_mul(rows_in[...], both)
        for owner in range(s.owners):
            held[owner, outer] = result[owner * s.block : (owner + 1) * s.block]
    out = [
        to_peer(
            "ga", step, held.at[targets[step]], landed.at[part_at, owner_at],
            send_sem.at[step - 1], recv_sem.at[step - 1],
        )
        for step in range(1, s.owners)
    ]
    for copy in out:
        copy.start()
    own = pltpu.make_async_copy(held.at[owner_at], landed.at[part_at, owner_at], local_sem.at[3])
    own.start()
    swaps = []
    for step in range(s.owners):
        if step:
            out[step - 1].wait_recv()
            source = landed.at[part_at, sources[step]]
        else:
            source = held.at[owner_at]
        swap = to_peer(
            "pert", 1, source, landed.at[part_at, sources[step]],
            swap_send.at[step], swap_recv.at[step],
        )
        swap.start()
        swaps.append(swap)
    fetch.wait()
    own.wait()
    for swap in swaps:
        swap.wait_recv()

    weights = (z_in, x_in, x_out, z_out)

    def early(at, step):
        return to_peer(
            "ga", step, back_held.at[0, targets[step], at], back_landed.at[0, owner_at, at],
            first_send.at[at, step - 1], first_recv.at[at, step - 1],
        )

    @pl.loop(0, s.chunks)
    def _(at):
        apply_rows(s, at, landed, pot_vmem, weights, back_held)
        for step in range(1, s.owners):
            early(at, step).start()

    late = [
        to_peer(
            "ga", step, back_held.at[1, targets[step]], back_landed.at[1, owner_at],
            back_send.at[step - 1], back_recv.at[step - 1],
        )
        for step in range(1, s.owners)
    ]
    for copy in late:
        copy.start()
    mine = [
        pltpu.make_async_copy(
            back_held.at[part, owner_at], back_landed.at[part, owner_at], back_own.at[part]
        )
        for part in range(s.parts)
    ]
    for copy in mine:
        copy.start()
    for part in range(s.parts):
        mine[part].wait()
        if part == 0:
            for at in range(s.chunks):
                for step in range(1, s.owners):
                    early(at, step).wait_recv()
        else:
            for copy in late:
                copy.wait_recv()
        for outer in range(s.outer):
            rows = jnp.concatenate(
                [
                    back_landed[part, owner, at, outer]
                    for owner in range(s.owners)
                    for at in range(s.chunks)
                ],
                axis=0,
            )
            both = jnp.concatenate([rows, turn(rows, s.kept)], axis=0)
            high, low = halves(left_mul(rows_out[...], both).T)
            table[:, outer * s.kept : (outer + 1) * s.kept] = high
            table[:, s.rows + outer * s.kept : s.rows + (outer + 1) * s.kept] = low
        gather(s, part, codes, iota_ref, table, out_ref)

    keep.wait()
    for copy in spread:
        copy.wait_recv()
    real, imag = out_ref[0], out_ref[1]
    pieces = []
    for band in range(bands):
        left_real, left_imag = basis[band, 0], basis[band, 1]
        pieces.append(jnp.sum(left_real * real + left_imag * imag, axis=0, keepdims=True))
        pieces.append(jnp.sum(left_real * imag - left_imag * real, axis=0, keepdims=True))
    sums[owner_at] = jnp.concatenate(pieces, axis=0)
    adds = [
        to_peer(
            "ga", step, sums.at[owner_at], sums.at[owner_at],
            sum_send.at[step - 1], sum_recv.at[step - 1],
        )
        for step in range(1, s.owners)
    ]
    for copy in adds:
        copy.start()
    for copy in adds:
        copy.wait_recv()
    total = sums[0]
    for owner in range(1, s.owners):
        total = total + sums[owner]
    total = jnp.sum(total, axis=1, keepdims=True) / float(s.points * s.owners)
    for band in range(bands):
        kept = occupied_ref[band].astype(F32)
        over_real = total[2 * band : 2 * band + 1] * kept
        over_imag = total[2 * band + 1 : 2 * band + 2] * kept
        left_real, left_imag = basis[band, 0], basis[band, 1]
        real = real - (left_real * over_real - left_imag * over_imag)
        imag = imag - (left_real * over_imag + left_imag * over_real)
    out_ref[0] = real
    out_ref[1] = imag
    for at in range(s.chunks):
        for step in range(1, s.owners):
            early(at, step).wait_send()
    for copy in spread + out + swaps + late + adds:
        copy.wait_send()


VMEM = pl.BlockSpec(memory_space=pltpu.VMEM)
SMEM = pl.BlockSpec(memory_space=pltpu.SMEM)
ANY = pl.BlockSpec(memory_space=pl.ANY)
DMA = pltpu.SemaphoreType.DMA


def shards(psi, potential, miller, occupied):
    s = Sizes(psi, potential, lax.axis_size("ga"))
    w = twiddles(s)
    bands = lax.axis_size("band")
    peers = s.owners - 1
    lines = s.points // LANES
    dense = (2, lines, LANES)
    names = ("rows_in", "z_in", "x_in", "x_out", "z_out", "rows_out")
    back = (s.parts, s.owners, s.chunks, s.outer, ROWS, s.width)
    out = pl.pallas_call(
        functools.partial(whole_kernel, s),
        out_shape=jax.ShapeDtypeStruct(dense, F32),
        in_specs=[ANY, VMEM, ANY, SMEM] + [VMEM] * len(names),
        out_specs=VMEM,
        scratch_shapes=[
            pltpu.VMEM((lines, LANES), jnp.int32),
            pltpu.VMEM(dense, jnp.int32),
            pltpu.VMEM((bands,) + dense, F32),
            pltpu.VMEM(potential.shape, F32),
            pltpu.VMEM((max(s.rows, s.groups * s.kept), s.chunk), BF16),
            pltpu.VMEM((s.rows, s.width), F32),
            pltpu.VMEM((s.owners, s.outer, s.block, s.width), F32),
            pltpu.VMEM((s.parts, s.owners, s.outer, s.block, s.width), F32),
            pltpu.VMEM(back, F32),
            pltpu.VMEM(back, F32),
            pltpu.VMEM((s.width, 2 * s.rows), BF16),
            pltpu.VMEM((s.owners, 2 * bands, LANES), F32),
            DMA((4,)),
            DMA((bands - 1,)), DMA((bands - 1,)),
            DMA((peers,)), DMA((peers,)),
            DMA((s.owners,)), DMA((s.owners,)),
            DMA((s.chunks, peers)), DMA((s.chunks, peers)), DMA((s.chunks,)),
            DMA((peers,)), DMA((peers,)), DMA((s.parts,)),
            DMA((peers,)), DMA((peers,)),
        ],
        compiler_params=pltpu.CompilerParams(
            vmem_limit_bytes=56 * 1024 * 1024, collective_id=0, has_side_effects=True
        ),
        name="whole",
    )(
        miller.reshape(-1, LANES), psi.reshape(dense), potential, occupied,
        *[w[name] for name in names],
    )
    return out.reshape(psi.shape)


highest = lax.Precision.HIGHEST


def phases(first_index, second_index, direction, length):
    turns = first_index[:, None] * second_index[None, :] % length
    angle = direction * 2.0 * jnp.pi / length * turns.astype(jnp.float32)
    return (jnp.cos(angle), jnp.sin(angle))


def contract(pattern, real_part, imag_part, twiddle):
    cosine, sine_part = twiddle
    out_real = jnp.einsum(pattern, real_part, cosine, precision=highest) - jnp.einsum(
        pattern, imag_part, sine_part, precision=highest
    )
    out_imag = jnp.einsum(pattern, real_part, sine_part, precision=highest) + jnp.einsum(
        pattern, imag_part, cosine, precision=highest
    )
    return (out_real, out_imag)


def inner_products(left_real, left_imag, right_real, right_imag):
    over_real = jnp.einsum("mk,nk->mn", left_real, right_real, precision=highest) + jnp.einsum(
        "mk,nk->mn", left_imag, right_imag, precision=highest
    )
    over_imag = jnp.einsum("mk,nk->mn", left_real, right_imag, precision=highest) - jnp.einsum(
        "mk,nk->mn", left_imag, right_real, precision=highest
    )
    return (over_real, over_imag)


def subtract(applied_real, applied_imag, basis_real, basis_imag, weight_real, weight_imag):
    proj_real = jnp.einsum("mn,mk->nk", weight_real, basis_real, precision=highest) - jnp.einsum(
        "mn,mk->nk", weight_imag, basis_imag, precision=highest
    )
    proj_imag = jnp.einsum("mn,mk->nk", weight_imag, basis_real, precision=highest) + jnp.einsum(
        "mn,mk->nk", weight_real, basis_imag, precision=highest
    )
    return (applied_real - proj_real, applied_imag - proj_imag)


def plain_shards(psi, potential, miller, occupied):
    grid_size = potential.shape[0]
    owners = lax.axis_size("ga")
    quarter = grid_size // 4
    per_shard = psi.shape[2]
    band_count = psi.shape[1]
    total = per_shard * lax.axis_size("ga")
    owner_index = lax.axis_index("ga")
    kept_rows = grid_size // 2
    kept_planes = grid_size // (2 * owners)
    full_index = jnp.arange(grid_size, dtype=jnp.int32)
    kept_index = (jnp.arange(kept_rows, dtype=jnp.int32) + grid_size - quarter) % grid_size
    inverse_rows = phases(kept_index, full_index, 1.0, grid_size)
    forward_rows = phases(full_index, kept_index, -1.0, grid_size)
    slot_index = jnp.arange(owners * kept_planes, dtype=jnp.int32)
    plane_index = (
        slot_index // kept_planes + owners * (slot_index % kept_planes) + grid_size - quarter
    ) % grid_size
    inverse_planes = phases(plane_index, full_index, 1.0, grid_size)
    forward_planes = phases(full_index, plane_index, -1.0, grid_size)
    local_points = lax.dynamic_slice_in_dim(miller, owner_index * per_shard, per_shard)
    index_a = local_points // (grid_size * grid_size)
    index_b = local_points // grid_size % grid_size
    index_c = local_points % grid_size
    plane_pos = (index_a + quarter) % grid_size
    position = (plane_pos // owners * kept_rows + (index_b + quarter) % grid_size) * kept_rows + (
        index_c + quarter
    ) % grid_size
    slab_size = kept_planes * kept_rows * kept_rows
    real_part = jnp.zeros((band_count, slab_size), jnp.float32).at[:, position].set(psi[0])
    imag_part = jnp.zeros((band_count, slab_size), jnp.float32).at[:, position].set(psi[1])
    real_part = real_part.reshape(band_count, kept_planes, kept_rows, kept_rows)
    imag_part = imag_part.reshape(band_count, kept_planes, kept_rows, kept_rows)
    real_part, imag_part = contract("ntbc,by->ntyc", real_part, imag_part, inverse_rows)
    pieces = (
        lax.all_to_all(real_part, "ga", split_axis=2, concat_axis=1, tiled=True),
        lax.all_to_all(imag_part, "ga", split_axis=2, concat_axis=1, tiled=True),
    )
    wide_real, wide_imag = contract("nsyc,cz->nsyz", pieces[0], pieces[1], inverse_rows)
    pieces = (wide_real, wide_imag)
    wave_real, wave_imag = contract("nsyz,sx->nxyz", pieces[0], pieces[1], inverse_planes)
    wave_real = wave_real * potential
    wave_imag = wave_imag * potential
    wide_real, wide_imag = contract("nxyz,xs->nsyz", wave_real, wave_imag, forward_planes)
    narrow = contract("nsyz,zc->nsyc", wide_real, wide_imag, forward_rows)
    real_part = lax.all_to_all(narrow[0], "ga", split_axis=1, concat_axis=2, tiled=True)
    imag_part = lax.all_to_all(narrow[1], "ga", split_axis=1, concat_axis=2, tiled=True)
    real_part, imag_part = contract("ntyc,yb->ntbc", real_part, imag_part, forward_rows)
    inverse_volume = 1.0 / grid_size**3
    applied_real = real_part.reshape(band_count, slab_size)[:, position] * inverse_volume
    applied_imag = imag_part.reshape(band_count, slab_size)[:, position] * inverse_volume
    weights = occupied.astype(jnp.float32)[:, None]
    moved_parts = (
        lax.all_to_all(applied_real, "band", split_axis=1, concat_axis=0, tiled=True),
        lax.all_to_all(applied_imag, "band", split_axis=1, concat_axis=0, tiled=True),
        lax.all_to_all(psi[0], "band", split_axis=1, concat_axis=0, tiled=True),
        lax.all_to_all(psi[1], "band", split_axis=1, concat_axis=0, tiled=True),
    )
    column_real, column_imag, basis_real, basis_imag = moved_parts
    over_real, over_imag = inner_products(basis_real, basis_imag, column_real, column_imag)
    over_real, over_imag = lax.psum((over_real, over_imag), ("ga", "band"))
    weight_real = weights * (over_real / total)
    weight_imag = weights * (over_imag / total)
    left_real, left_imag = subtract(
        column_real, column_imag, basis_real, basis_imag, weight_real, weight_imag
    )
    left_real, left_imag = (
        lax.all_to_all(left_real, "band", split_axis=0, concat_axis=1, tiled=True),
        lax.all_to_all(left_imag, "band", split_axis=0, concat_axis=1, tiled=True),
    )
    return jnp.stack([left_real, left_imag])


def solution(mesh):
    def body(psi, potential, miller, occupied):
        if potential.shape[1] % ROWS or lax.axis_size("pert") != 2:
            return plain_shards(psi, potential, miller, occupied)
        return shards(psi, potential, miller, occupied)

    in_specs = (P(None, "band", "ga"), P("pert", "ga", None), P(), P())
    out_specs = P(None, ("pert", "band"), "ga")
    return jax.shard_map(body, mesh=mesh, in_specs=in_specs, out_specs=out_specs, check_vma=False)
```
